128 devices in a mesh: row: 8 (over y_lo, z), head: 16 (over y_hi, x, core).
Axes of the slice: x: 4, y: 4 (y_hi: 2, y_lo: 2; y = y_hi * 2 + y_lo), z: 4, core: 2. Of those that a mesh axis runs over, the one named last changes fastest.
Arguments:
- tokens: bfloat16 [12288, 4096], P('row', 'head'), may hold values from -500 to 500
- norm_gain: float32 [4096], replicated, may hold values from 0.1 to 1.9
- projection: bfloat16 [4096, 4, 4096], P(None, None, 'head'), may hold values from -0.09375 to 0.09375
- lengths: int32 [8, 12], replicated, may hold values from 1 to 256, 1536 in all within a row
- sample_passage: int32 [192], replicated, may hold values from 0 to 95, as said below
Outputs:
- cross_cache: bfloat16 [192, 256, 4, 4096], P('row', None, None, 'head')
The draws below stay inside these ranges and needn't reach their ends.
Inputs may be any that keep to these rules, and one draw needn't show every extreme that they name: Every row of lengths sums to 1536; each row's largest entry is exactly 256. `sample_passage`: every passage is named by at least one sample row.
All inputs are finite; a program needn't handle non-finite values.
Results may differ from the reference program's by a relative error of at most 0.005.
Values may be sent and summed in bfloat16 or wider, within the bound.
A program may use at most 192 MiB of HBM per device.

```python
import math
import jax
import jax.numpy as jnp
import numpy as np
from jax import lax

D = 4096
PLEN = 256
PASS_DEV = 12
INNER = 4096
KV = 4
TOK_DEV = 1536
SHARDS = 8
TOKENS = 12288
PASSAGES = 96
SAMPLES = 192


def draw_tokens(key, part):
    key_base, key_cols, key_rows = jax.random.split(jax.random.fold_in(key, 11), 3)
    column_pos = jnp.arange(D, dtype=jnp.float32) / D
    column_scale = jnp.exp(jnp.log(3.0) * column_pos + jax.random.uniform(key_cols, (D,), jnp.float32, 0.0, jnp.log(4.0)))
    row_scale = jnp.exp(jax.random.uniform(key_rows, (TOKENS, 1), jnp.float32, 0.0, jnp.log(10.0)))
    base_values = jax.random.normal(key_base, (TOKENS, D), jnp.float32)
    base_values = jnp.clip(base_values, -4.0, 4.0)
    return (base_values * column_scale[None, :] * row_scale).astype(jnp.bfloat16)


def draw_sample_passage(key, part):
    key_hot, key_pick, key_label, key_order = jax.random.split(jax.random.fold_in(key, 23), 4)
    extra_count = SAMPLES - PASSAGES
    hot_limit = jax.random.randint(key_hot, (extra_count,), 1, PASSAGES + 1)
    extra_ids = jax.random.randint(key_pick, (extra_count,), 0, hot_limit)
    combined = jnp.concatenate([jnp.arange(PASSAGES, dtype=jnp.int32), extra_ids.astype(jnp.int32)])
    relabel = jax.random.permutation(key_label, PASSAGES).astype(jnp.int32)
    labelled = relabel[combined]
    ordering = jax.random.permutation(key_order, SAMPLES)
    return labelled[ordering].astype(jnp.int32)


def shard_levels(own_key, dims, pieces, smallest, high):
    def one(position, blocks):
        draws = jax.random.uniform(jax.random.fold_in(jax.random.fold_in(own_key, 6), position), (blocks,), jnp.float32, smallest / len(pieces), high / len(pieces))
        return jnp.repeat(jnp.exp(draws), dims[position] // blocks).reshape((-1,) + (1,) * (len(dims) - position - 1))

    gain = one(*pieces[0])
    for cut in pieces[1:]:
        gain = gain * one(*cut)
    return gain


def profile(number_of, total, reach, skew):
    weights = [(1 << 20) // math.isqrt(standing ** skew) + 1 for standing in range(2, number_of + 1)]
    spare, given = total - reach - (number_of - 1), [1] * (number_of - 1)
    while spare > 0:
        candidates = [i for i in range(number_of - 1) if given[i] < reach]
        pool, budget = sum([weights[i] for i in candidates]), spare
        for i in candidates:
            extra = min(reach - given[i], max(1, budget * weights[i] // pool), spare)
            given[i] = given[i] + extra
            spare = spare - extra
    return np.array([reach] + given)


def uneven_parts(stream_key, amount, total, bound, lean):
    if amount == 2:
        one = jax.random.randint(stream_key, (), max(1, total - bound), min(bound, total - 1) + 1)
        return jnp.stack([one, total - one])
    sizes = jnp.asarray(profile(amount, total, bound, lean), jnp.int32)
    twos = (amount - 1) // 2
    donor, taker = sizes[1:1 + 2 * twos:2], sizes[2:2 + 2 * twos:2]
    room = jnp.minimum(donor - 1, bound - taker)
    moved = jax.random.randint(jax.random.fold_in(stream_key, 1), (twos,), 0, 1 << 20) % (room + 1)
    sizes = sizes.at[1:1 + 2 * twos:2].set(donor - moved).at[2:2 + 2 * twos:2].set(taker + moved)
    return sizes[jax.random.permutation(jax.random.fold_in(stream_key, 2), amount)]


def bell_draw(rng, extent, deviation, reach, cuts=(), held_as=jnp.bfloat16):
    entries = deviation * jax.random.normal(rng, extent, jnp.float32)
    if cuts:
        entries = entries * shard_levels(rng, extent, cuts, -0.22, 0.18)
    return jnp.clip(entries, -reach, reach).astype(held_as)


def setup_inputs(seed: int = 0) -> dict:
    key_of = jax.random.split(jax.random.key(seed), 6)
    return {
        "tokens": draw_tokens(jax.random.fold_in(key_of[5], 71), 0),
        "norm_gain": jnp.clip(1.0 + 0.18 * jax.random.normal(key_of[1], (D,), jnp.float32), 0.1, 1.9),
        "projection": bell_draw(key_of[2], (D, KV, INNER), D ** -0.5, 0.09375, ((2, 16),)),
        "lengths": jax.vmap(lambda own: uneven_parts(own, PASS_DEV, TOK_DEV, PLEN, 2))(jax.random.split(key_of[3], SHARDS)).reshape((SHARDS, PASS_DEV)).astype(jnp.int32),
        "sample_passage": draw_sample_passage(jax.random.fold_in(key_of[5], 71), 0),
    }


epsilon = 1e-06

def reference(tokens, norm_gain, projection, lengths, sample_passage):
    widened = tokens.astype(jnp.float32)
    inverse = lax.rsqrt(lax.optimization_barrier(jnp.mean(widened * widened, axis=1, keepdims=True)) + epsilon)
    normed = (widened * inverse * norm_gain).astype(jnp.bfloat16)
    flat_weight = projection.reshape(D, KV * INNER)
    projected = jnp.dot(normed, flat_weight, preferred_element_type=jnp.float32).astype(jnp.bfloat16)
    projected = projected.reshape(TOKENS, KV, INNER)
    block_base = (jnp.arange(SHARDS, dtype=jnp.int32) * TOK_DEV)[:, None]
    offsets = (jnp.cumsum(lengths, axis=1) - lengths + block_base).reshape(-1).astype(jnp.int32)
    flat_lengths = lengths.reshape(-1).astype(jnp.int32)
    first_token = offsets[sample_passage]
    passage_len = flat_lengths[sample_passage]
    positions = jnp.arange(PLEN, dtype=jnp.int32)
    token_index = jnp.clip(first_token[:, None] + positions[None, :], 0, TOKENS - 1).astype(jnp.int32)
    filled = positions[None, :] < passage_len[:, None]
    picked = projected[token_index]
    return jnp.where(filled[:, :, None, None], picked, jnp.zeros_like(picked)).astype(jnp.bfloat16)
```

```python
import functools

import jax
import jax.numpy as jnp
from jax import lax
from jax.experimental import pallas as pl
from jax.experimental.pallas import tpu as pltpu
from jax.sharding import PartitionSpec as P

PLEN = 256
epsilon = 1e-06
MESH = pl.DeviceIdType.MESH
VMEM = pltpu.VMEM
UNITS = 8
GROUP = 8
SIZES = (3072, 3328, 3584, 3840)


def gather_project(units, idx, tokens, weight, gain, kv, raw_a, raw_b, spread, matrix, partial, stage, packed,
                   load_sem, send1, recv1, send2, recv2, out_sem):
    raws = (raw_a, raw_b)
    rows_all = spread.shape[3]
    count = rows_all // units
    half_count = count // 2
    groups = tokens.shape[0]
    steps = 2 * units
    row = lax.axis_index("row")
    head = lax.axis_index("head")
    y_lo, z = row // 4, row % 4
    core = head % 2
    yx = head // 2
    y_hi, x = yx // 4, yx % 4
    y_other = (1 - y_lo) * 4
    z_up, z_down, z_far = (z + 1) % 4, (z + 3) % 4, (z + 2) % 4
    x_up, x_down, x_far = (x + 1) % 4, (x + 3) % 4, (x + 2) % 4
    h_mine, h_other = y_hi * 4, (1 - y_hi) * 4

    to_y = (y_other + z, head)
    to_zu = (y_lo * 4 + z_up, head)
    to_zd = (y_lo * 4 + z_down, head)
    to_yy = (row, (h_other + x) * 2 + core)
    to_xu = (row, (h_mine + x_up) * 2 + core)
    to_xd = (row, (h_mine + x_down) * 2 + core)
    to_sib = (row, yx * 2 + 1 - core)

    barrier = pltpu.get_barrier_semaphore()
    for peer in (to_y, to_zu, to_zd, to_yy, to_xu, to_xd, to_sib):
        pl.semaphore_signal(barrier, inc=1, device_id=peer, device_id_type=MESH)

    def load(h):
        return pltpu.make_async_copy(tokens.at[:, :, pl.ds(h * 128, 128)], raws[h].at[pl.ds(row * groups, groups)],
                                     load_sem.at[h])

    load(0).start()
    load(1).start()

    def block(h, r, part=None):
        if part is None:
            return raws[h].at[pl.ds(r * groups, groups)]
        return raws[h].at[pl.ds(r * groups + part * (groups // 2), groups // 2)]

    def first(h, kind, ref, to):
        return pltpu.make_async_remote_copy(src_ref=ref, dst_ref=ref, send_sem=send1.at[h, kind],
                                            recv_sem=recv1.at[h, kind], device_id=to, device_id_type=MESH)

    def first_out(h):
        mine = block(h, row)
        other = block(h, y_other + z)
        return [
            (mine, to_y), (mine, to_zu), (mine, to_zd), (other, to_zu), (other, to_zd),
            (block(h, y_lo * 4 + z_down, 0), to_zu), (block(h, y_lo * 4 + z_up, 1), to_zd),
            (block(h, y_lo * 4 + z_far), to_y),
        ]

    def first_in(h):
        return [
            block(h, y_other + z), block(h, y_lo * 4 + z_down), block(h, y_lo * 4 + z_up), block(h, y_other + z_down),
            block(h, y_other + z_up), block(h, y_lo * 4 + z_far, 0), block(h, y_lo * 4 + z_far, 1),
            block(h, y_other + z_far),
        ]

    def first_start(h, *kinds):
        out = first_out(h)
        for kind in kinds:
            first(h, kind, *out[kind]).start()

    def first_wait(h, *kinds):
        got = first_in(h)
        for kind in kinds:
            first(h, kind, got[kind], to_y).wait_recv()

    blocks = weight.shape[0] // 256

    def fetch(i):
        return pltpu.make_async_copy(weight.at[pl.ds(i * 256, 256)], stage.at[i % 2], load_sem.at[2 + i % 2])

    fetch(0).start()

    def prepare(i, carry):
        @pl.when(i + 1 < blocks)
        def _():
            fetch(i + 1).start()

        fetch(i).wait()
        block_now = stage[i % 2]
        for h in range(2):
            scale = jnp.broadcast_to(gain[pl.ds(2 * i + h, 1), :], (128, 128)).T
            scale = jnp.concatenate([scale, scale], axis=1)
            for c in range(4):
                part = block_now[h * 128:h * 128 + 128, c, :].astype(jnp.float32) * scale
                matrix[h, pl.ds(pl.multiple_of(i * 128, 128), 128), c * 256:c * 256 + 256] = part.astype(jnp.bfloat16)
        return carry

    def slab(h, c, p, u, part=None):
        if part is None:
            return spread.at[h, c, p, pl.ds(pl.multiple_of(u * count, 32), count)]
        return spread.at[h, c, p, pl.ds(pl.multiple_of(u * count + part * half_count, 16), half_count)]

    def second(t, kind, ref, to):
        return pltpu.make_async_remote_copy(src_ref=ref, dst_ref=ref, send_sem=send2.at[t, kind],
                                            recv_sem=recv2.at[t, kind], device_id=to, device_id_type=MESH)

    def both(h, c, u):
        return spread.at[h, c, :, pl.ds(pl.multiple_of(u * count, 32), count)]

    def second_out(t):
        h, u = t // units, t % units
        mine = slab(h, core, yx, u)
        other = slab(h, core, h_other + x, u)
        return [
            (mine, to_yy), (mine, to_xu), (mine, to_xd), (other, to_xu), (other, to_xd),
            (slab(h, core, h_mine + x_down, u, 0), to_xu), (slab(h, core, h_mine + x_up, u, 1), to_xd),
            (slab(h, core, h_mine + x_far, u), to_yy), (both(h, core, u), to_sib),
        ]

    def second_in(t):
        h, u = t // units, t % units
        return [
            slab(h, core, h_other + x, u), slab(h, core, h_mine + x_down, u), slab(h, core, h_mine + x_up, u),
            slab(h, core, h_other + x_down, u), slab(h, core, h_other + x_up, u), slab(h, core, h_mine + x_far, u, 0),
            slab(h, core, h_mine + x_far, u, 1), slab(h, core, h_other + x_far, u), both(h, 1 - core, u),
        ]

    def second_start(t, *kinds):
        out = second_out(t)
        for kind in kinds:
            second(t, kind, *out[kind]).start()

    def second_wait(t, *kinds):
        got = second_in(t)
        for kind in kinds:
            second(t, kind, got[kind], to_yy).wait_recv()

    def pick(h, u):
        def two(k, carry):
            g = u * (count // GROUP) + 2 * k
            pair = jnp.concatenate([raws[h][idx[g]], raws[h][idx[g + 1]]], axis=0)
            spread[h, core, yx, pl.ds(pl.multiple_of(u * count + k * 16, 16), 16), :] = pair
            return carry

        lax.fori_loop(0, count // 16, two, 0, unroll=2)

    def store(u):
        return pltpu.make_async_copy(packed.at[u % 2], kv.at[pl.ds(u * count, count)], out_sem.at[u % 2])

    def multiply(h, u):
        if h == 1:
            @pl.when(u >= 2)
            def _():
                store(u - 2).wait()

        def piece(k, carry):
            rows = pl.ds(pl.multiple_of(u * count + k * half_count, 16), half_count)
            parts = [spread[h, j % 2, j // 2, rows, :] for j in range(16)]
            left = jnp.concatenate(parts, axis=1)
            if h == 0:
                for c in range(4):
                    cols = slice(c * 256, c * 256 + 256)
                    value = jnp.dot(left, matrix[0, :, cols], preferred_element_type=jnp.float32)
                    partial[rows, cols] = value.astype(jnp.bfloat16)
                return carry
            total = jnp.zeros((half_count, 128), jnp.float32)
            for part in parts + [spread[0, j % 2, j // 2, rows, :] for j in range(16)]:
                wide = part.astype(jnp.float32)
                total = total + wide * wide
            inverse = lax.rsqrt(jnp.sum(total, axis=1, keepdims=True) / (32.0 * 128.0) + epsilon)
            outs = []
            for c in range(4):
                cols = slice(c * 256, c * 256 + 256)
                value = jnp.dot(left, matrix[1, :, cols], preferred_element_type=jnp.float32)
                value = value + partial[rows, cols].astype(jnp.float32)
                outs.append((value * inverse).astype(jnp.bfloat16))
            packed[u % 2, pl.ds(pl.multiple_of(k * half_count, 16), half_count)] = jnp.stack(outs, axis=1)
            return carry

        lax.fori_loop(0, 2, piece, 0)
        if h == 1:
            store(u).start()

    load(0).wait()
    pl.semaphore_wait(barrier, 7)
    first_start(0, 0, 1, 2)
    lax.fori_loop(0, 7, prepare, 0)
    first_wait(0, 1, 2)
    first_start(0, 5, 6)
    first_wait(0, 0)
    first_start(0, 3, 4)
    load(1).wait()
    first_start(1, 0, 1, 2)
    lax.fori_loop(7, 11, prepare, 0)
    first_wait(0, 5, 6)
    first_start(0, 7)
    lax.fori_loop(11, blocks, prepare, 0)
    first_wait(0, 3, 4, 7)
    pick(0, 0)
    second_start(0, 0, 1, 2)

    def step(t, carry):
        @pl.when(t == 1)
        def _():
            first_wait(1, 1, 2)
            first_start(1, 5, 6)
            first_wait(1, 0)
            first_start(1, 3, 4)

        @pl.when(t == 3)
        def _():
            first_wait(1, 5, 6)
            first_start(1, 7)

        @pl.when(t + 1 < units)
        def _():
            pick(0, t + 1)

        @pl.when(t + 1 == units)
        def _():
            first_wait(1, 3, 4, 7)

        @pl.when((t + 1 >= units) & (t + 1 < steps))
        def _():
            pick(1, t + 1 - units)

        @pl.when(t + 1 < steps)
        def _():
            second_start(t + 1, 0, 1, 2)

        @pl.when(t < steps)
        def _():
            second_wait(t, 1, 2)
            second_start(t, 5, 6)
            second_wait(t, 0)
            second_start(t, 3, 4)

        @pl.when((t >= 1) & (t < steps + 1))
        def _():
            second_wait(t - 1, 5, 6)
            second_start(t - 1, 7)

        @pl.when((t >= 2) & (t < steps + 2))
        def _():
            second_wait(t - 2, 3, 4, 7)
            second_start(t - 2, 8)

        @pl.when((t >= 3) & (t < units + 3))
        def _():
            second_wait(t - 3, 8)
            multiply(0, t - 3)

        @pl.when(t >= units + 3)
        def _():
            second_wait(t - 3, 8)
            multiply(1, t - 3 - units)

        return carry

    lax.fori_loop(0, steps + 3, step, 0)
    store(units - 2).wait()
    store(units - 1).wait()
    for h in range(2):
        for kind, (ref, to) in enumerate(first_out(h)):
            first(h, kind, ref, to).wait_send()

    def finish(t, carry):
        for kind, (ref, to) in enumerate(second_out(t)):
            second(t, kind, ref, to).wait_send()
        return carry

    lax.fori_loop(0, steps, finish, 0)


def run_gather_project(size, order, idx, tokens, weight, gain):
    row_count = lax.axis_size("row")
    groups = tokens.shape[0]
    count = size // UNITS
    width = weight.shape[1] * weight.shape[2]
    depth = weight.shape[0]
    return pl.pallas_call(
        functools.partial(gather_project, UNITS),
        out_shape=jax.ShapeDtypeStruct((size,) + weight.shape[1:], jnp.bfloat16),
        in_specs=[
            pl.BlockSpec(memory_space=pltpu.SMEM),
            pl.BlockSpec(memory_space=pl.ANY),
            pl.BlockSpec(memory_space=pl.ANY),
            pl.BlockSpec(memory_space=VMEM),
        ],
        out_specs=pl.BlockSpec(memory_space=pl.ANY),
        scratch_shapes=[
            VMEM((row_count * groups, GROUP, 128), jnp.bfloat16),
            VMEM((row_count * groups, GROUP, 128), jnp.bfloat16),
            VMEM((2, 2, 8, size, 128), jnp.bfloat16),
            VMEM((2, depth // 2, width), jnp.bfloat16),
            VMEM((size, width), jnp.bfloat16),
            VMEM((2, 256) + weight.shape[1:], jnp.bfloat16),
            VMEM((2, count) + weight.shape[1:], jnp.bfloat16),
            pltpu.SemaphoreType.DMA((4,)),
            pltpu.SemaphoreType.DMA((2, 8)),
            pltpu.SemaphoreType.DMA((2, 8)),
            pltpu.SemaphoreType.DMA((2 * UNITS, 9)),
            pltpu.SemaphoreType.DMA((2 * UNITS, 9)),
            pltpu.SemaphoreType.DMA((2,)),
        ],
        compiler_params=pltpu.CompilerParams(
            collective_id=order, has_side_effects=True, vmem_limit_bytes=60 * 2**20),
        name=f"gather_project_{size}",
    )(idx, tokens, weight, gain)


def lay_out(begin, length, kv, out, zeros, sem, zero_sem):
    samples, plen = out.shape[0], out.shape[1]
    zeros[...] = jnp.zeros_like(zeros)

    def rows(s):
        n = length[s]
        return pltpu.make_async_copy(kv.at[pl.ds(begin[s], n)], out.at[s, pl.ds(0, n)], sem.at[s])

    def rest(s):
        n = length[s]
        return pltpu.make_async_copy(zeros.at[pl.ds(0, plen - n)], out.at[s, pl.ds(n, plen - n)], zero_sem.at[s])

    for s in range(samples):
        rows(s).start()

        @pl.when(length[s] < plen)
        def _():
            rest(s).start()

    for s in range(samples):
        rows(s).wait()

        @pl.when(length[s] < plen)
        def _():
            rest(s).wait()


def run_lay_out(begin, length, kv):
    samples = begin.shape[0]
    return pl.pallas_call(
        lay_out,
        out_shape=jax.ShapeDtypeStruct((samples, PLEN) + kv.shape[1:], kv.dtype),
        in_specs=[
            pl.BlockSpec(memory_space=pltpu.SMEM),
            pl.BlockSpec(memory_space=pltpu.SMEM),
            pl.BlockSpec(memory_space=pl.ANY),
        ],
        out_specs=pl.BlockSpec(memory_space=pl.ANY),
        scratch_shapes=[
            VMEM((PLEN,) + kv.shape[1:], kv.dtype),
            pltpu.SemaphoreType.DMA((samples,)),
            pltpu.SemaphoreType.DMA((samples,)),
        ],
        name="lay_out",
    )(begin, length, kv)


def any_size(tokens, norm_gain, projection, wanted, first_token, passage_len):
    rows_here, columns = tokens.shape
    model_width = columns * lax.axis_size("head")
    pair_count, inner_dev = (projection.shape[1], projection.shape[2])
    flat_weight = projection.reshape(model_width, pair_count * inner_dev)
    gathered = lax.all_gather(tokens, "head", axis=1, tiled=True)
    widened = gathered.astype(jnp.float32)
    inverse = lax.rsqrt(jnp.mean(widened * widened, axis=1, keepdims=True) + epsilon)
    normed = (widened * inverse * norm_gain[None, :]).astype(jnp.bfloat16)
    projected = jnp.dot(normed, flat_weight, preferred_element_type=jnp.float32)
    kv_rows = projected.astype(jnp.bfloat16).reshape(rows_here, pair_count, inner_dev)
    everything = lax.all_gather(kv_rows, "row", axis=0, tiled=True)
    positions = jnp.arange(PLEN, dtype=jnp.int32)
    target = first_token[:, None] + positions[None, :]
    filled = positions[None, :] < passage_len[:, None]
    picked = jnp.take(everything, jnp.clip(target, 0, everything.shape[0] - 1), axis=0)
    return jnp.where(filled[:, :, None, None], picked, jnp.zeros((), jnp.bfloat16))


def shards(tokens, norm_gain, projection, lengths, sample_passage):
    rows_here, columns = tokens.shape
    row_count = lax.axis_size("row")
    row_index = lax.axis_index("row")
    samp_here = sample_passage.shape[0] // row_count
    block_count, per_block = lengths.shape
    passages = block_count * per_block

    starts = jnp.cumsum(lengths, axis=1) - lengths
    block_base = (jnp.arange(block_count, dtype=jnp.int32) * rows_here)[:, None]
    offset = (starts + block_base).reshape(-1)
    length = lengths.reshape(-1)
    group_first = offset // GROUP
    group_last = (offset + length - 1) // GROUP
    order = jnp.arange(passages, dtype=jnp.int32)
    wanted = sample_passage.reshape(row_count, samp_here)
    flags = jnp.any(wanted[:, :, None] == order[None, None, :], axis=1)
    before = order[None, :] < order[:, None]
    covered = jnp.max(jnp.where(flags[:, None, :] & before[None], group_last[None, None, :], -1), axis=2)
    begin = jnp.maximum(group_first[None, :], covered + 1)
    number = jnp.where(flags, jnp.maximum(group_last[None, :] - begin + 1, 0), 0)
    ahead = jnp.sum(jnp.where(before[None], number[:, None, :], 0), axis=2)
    most = jnp.max(jnp.sum(number, axis=1)) * GROUP

    pick_row = jnp.arange(row_count, dtype=jnp.int32) == row_index

    def own(table):
        return jnp.sum(jnp.where(pick_row[:, None], table, 0), axis=0)

    number_own, ahead_own, begin_own, covered_own, wanted_own = (
        own(number), own(ahead), own(begin), own(covered), own(wanted))
    slot = jnp.arange(SIZES[-1] // GROUP, dtype=jnp.int32)[:, None]
    here = (slot >= ahead_own[None, :]) & (slot < (ahead_own + number_own)[None, :])
    idx = jnp.sum(jnp.where(here, begin_own[None, :] + slot - ahead_own[None, :], 0), axis=1)
    place = (ahead_own - (covered_own >= group_first).astype(jnp.int32)) * GROUP + offset % GROUP
    match = wanted_own[:, None] == order[None, :]

    def of_sample(table):
        return jnp.sum(jnp.where(match, table[None, :], 0), axis=1)

    first_row, first_token, passage_len = of_sample(place), of_sample(offset), of_sample(length)

    def sized(number_of, size):
        def branch():
            kv = run_gather_project(size, number_of, idx[:size // GROUP], tokens.reshape(-1, GROUP, columns), projection,
                                    norm_gain.reshape(-1, 128))
            return run_lay_out(first_row, passage_len, kv)

        return branch

    def rest():
        return any_size(tokens, norm_gain, projection, wanted_own, first_token, passage_len)

    branches = [sized(i, size) for i, size in enumerate(SIZES)] + [rest]
    tier = jnp.sum(jnp.array(SIZES, jnp.int32) < most)
    return lax.switch(tier, branches)


def solution(mesh):
    in_specs = (P("row", "head"), P(), P(None, None, "head"), P(), P())
    out_specs = P("row", None, None, "head")
    return jax.shard_map(shards, mesh=mesh, in_specs=in_specs, out_specs=out_specs, check_vma=False)
```

```python
import functools

import jax
import jax.numpy as jnp
from jax import lax
from jax.experimental import pallas as pl
from jax.experimental.pallas import tpu as pltpu
from jax.sharding import PartitionSpec as P

PLEN = 256
epsilon = 1e-06
MESH = pl.DeviceIdType.MESH
VMEM = pltpu.VMEM
UNITS = 8
GROUP = 8
SIZES = (3072, 3328, 3584, 3840)


def gather_project(units, idx, tokens, weight, gain, kv, raw_a, raw_b, spread, matrix, partial, stage, packed,
                   load_sem, send1, recv1, send2, recv2, out_sem):
    raws = (raw_a, raw_b)
    rows_all = spread.shape[3]
    count = rows_all // units
    half_count = count // 2
    groups = tokens.shape[0]
    steps = 2 * units
    row = lax.axis_index("row")
    head = lax.axis_index("head")
    y_lo, z = row // 4, row % 4
    core = head % 2
    yx = head // 2
    y_hi, x = yx // 4, yx % 4
    y_other = (1 - y_lo) * 4
    z_up, z_down, z_far = (z + 1) % 4, (z + 3) % 4, (z + 2) % 4
    x_up, x_down, x_far = (x + 1) % 4, (x + 3) % 4, (x + 2) % 4
    h_mine, h_other = y_hi * 4, (1 - y_hi) * 4

    to_y = (y_other + z, head)
    to_zu = (y_lo * 4 + z_up, head)
    to_zd = (y_lo * 4 + z_down, head)
    to_yy = (row, (h_other + x) * 2 + core)
    to_xu = (row, (h_mine + x_up) * 2 + core)
    to_xd = (row, (h_mine + x_down) * 2 + core)
    to_sib = (row, yx * 2 + 1 - core)

    barrier = pltpu.get_barrier_semaphore()
    for peer in (to_y, to_zu, to_zd, to_yy, to_xu, to_xd, to_sib):
        pl.semaphore_signal(barrier, inc=1, device_id=peer, device_id_type=MESH)

    def load(h):
        return pltpu.make_async_copy(tokens.at[:, :, pl.ds(h * 128, 128)], raws[h].at[pl.ds(row * groups, groups)],
                                     load_sem.at[h])

    load(0).start()
    load(1).start()

    def block(h, r, part=None):
        if part is None:
            return raws[h].at[pl.ds(r * groups, groups)]
        return raws[h].at[pl.ds(r * groups + part * (groups // 2), groups // 2)]

    def first(h, kind, ref, to):
        return pltpu.make_async_remote_copy(src_ref=ref, dst_ref=ref, send_sem=send1.at[h, kind],
                                            recv_sem=recv1.at[h, kind], device_id=to, device_id_type=MESH)

    def first_out(h):
        mine = block(h, row)
        other = block(h, y_other + z)
        return [
            (mine, to_y), (mine, to_zu), (mine, to_zd), (other, to_zu), (other, to_zd),
            (block(h, y_lo * 4 + z_down, 0), to_zu), (block(h, y_lo * 4 + z_up, 1), to_zd),
            (block(h, y_lo * 4 + z_far), to_y),
        ]

    def first_in(h):
        return [
            block(h, y_other + z), block(h, y_lo * 4 + z_down), block(h, y_lo * 4 + z_up), block(h, y_other + z_down),
            block(h, y_other + z_up), block(h, y_lo * 4 + z_far, 0), block(h, y_lo * 4 + z_far, 1),
            block(h, y_other + z_far),
        ]

    def first_start(h, *kinds):
        out = first_out(h)
        for kind in kinds:
            first(h, kind, *out[kind]).start()

    def first_wait(h, *kinds):
        got = first_in(h)
        for kind in kinds:
            first(h, kind, got[kind], to_y).wait_recv()

    blocks = weight.shape[0] // 256

    def fetch(i):
        return pltpu.make_async_copy(weight.at[pl.ds(i * 256, 256)], stage.at[i % 2], load_sem.at[2 + i % 2])

    fetch(0).start()

    def prepare(i, carry):
        @pl.when(i + 1 < blocks)
        def _():
            fetch(i + 1).start()

        fetch(i).wait()
        block_now = stage[i % 2]
        for h in range(2):
            scale = jnp.broadcast_to(gain[pl.ds(2 * i + h, 1), :], (128, 128)).T
            scale = jnp.concatenate([scale, scale], axis=1)
            for c in range(4):
                part = block_now[h * 128:h * 128 + 128, c, :].astype(jnp.float32) * scale
                matrix[h, pl.ds(pl.multiple_of(i * 128, 128), 128), c * 256:c * 256 + 256] = part.astype(jnp.bfloat16)
        return carry

    def slab(h, c, p, u, part=None):
        if part is None:
            return spread.at[h, c, p, pl.ds(pl.multiple_of(u * count, 32), count)]
        return spread.at[h, c, p, pl.ds(pl.multiple_of(u * count + part * half_count, 16), half_count)]

    def second(t, kind, ref, to):
        return pltpu.make_async_remote_copy(src_ref=ref, dst_ref=ref, send_sem=send2.at[t, kind],
                                            recv_sem=recv2.at[t, kind], device_id=to, device_id_type=MESH)

    def both(h, c, u):
        return spread.at[h, c, :, pl.ds(pl.multiple_of(u * count, 32), count)]

    def second_out(t):
        h, u = t // units, t % units
        mine = slab(h, core, yx, u)
        other = slab(h, core, h_other + x, u)
        return [
            (mine, to_yy), (mine, to_xu), (mine, to_xd), (other, to_xu), (other, to_xd),
            (slab(h, core, h_mine + x_down, u, 0), to_xu), (slab(h, core, h_mine + x_up, u, 1), to_xd),
            (slab(h, core, h_mine + x_far, u), to_yy), (both(h, core, u), to_sib),
        ]

    def second_in(t):
        h, u = t // units, t % units
        return [
            slab(h, core, h_other + x, u), slab(h, core, h_mine + x_down, u), slab(h, core, h_mine + x_up, u),
            slab(h, core, h_other + x_down, u), slab(h, core, h_other + x_up, u), slab(h, core, h_mine + x_far, u, 0),
            slab(h, core, h_mine + x_far, u, 1), slab(h, core, h_other + x_far, u), both(h, 1 - core, u),
        ]

    def second_start(t, *kinds):
        out = second_out(t)
        for kind in kinds:
            second(t, kind, *out[kind]).start()

    def second_wait(t, *kinds):
        got = second_in(t)
        for kind in kinds:
            second(t, kind, got[kind], to_yy).wait_recv()

    def pick(h, u):
        def two(k, carry):
            g = u * (count // GROUP) + 2 * k
            pair = jnp.concatenate([raws[h][idx[g]], raws[h][idx[g + 1]]], axis=0)
            spread[h, core, yx, pl.ds(pl.multiple_of(u * count + k * 16, 16), 16), :] = pair
            return carry

        lax.fori_loop(0, count // 16, two, 0, unroll=2)

    def store(u):
        return pltpu.make_async_copy(packed.at[u % 2], kv.at[pl.ds(u * count, count)], out_sem.at[u % 2])

    def multiply(h, u):
        if h == 1:
            @pl.when(u >= 2)
            def _():
                store(u - 2).wait()

        def piece(k, carry):
            rows = pl.ds(pl.multiple_of(u * count + k * half_count, 16), half_count)
            parts = [spread[h, j % 2, j // 2, rows, :] for j in range(16)]
            left = jnp.concatenate(parts, axis=1)
            if h == 0:
                for c in range(4):
                    cols = slice(c * 256, c * 256 + 256)
                    value = jnp.dot(left, matrix[0, :, cols], preferred_element_type=jnp.float32)
                    partial[rows, cols] = value.astype(jnp.bfloat16)
                return carry
            total = jnp.zeros((half_count, 128), jnp.float32)
            for part in parts + [spread[0, j % 2, j // 2, rows, :] for j in range(16)]:
                wide = part.astype(jnp.float32)
                total = total + wide * wide
            inverse = lax.rsqrt(jnp.sum(total, axis=1, keepdims=True) / (32.0 * 128.0) + epsilon)
            outs = []
            for c in range(4):
                cols = slice(c * 256, c * 256 + 256)
                value = jnp.dot(left, matrix[1, :, cols], preferred_element_type=jnp.float32)
                value = value + partial[rows, cols].astype(jnp.float32)
                outs.append((value * inverse).astype(jnp.bfloat16))
            packed[u % 2, pl.ds(pl.multiple_of(k * half_count, 16), half_count)] = jnp.stack(outs, axis=1)
            return carry

        lax.fori_loop(0, 2, piece, 0)
        if h == 1:
            store(u).start()

    load(0).wait()
    pl.semaphore_wait(barrier, 7)
    first_start(0, 0, 1, 2)
    lax.fori_loop(0, 7, prepare, 0)
    first_wait(0, 1, 2)
    first_start(0, 5, 6)
    first_wait(0, 0)
    first_start(0, 3, 4)
    load(1).wait()
    first_start(1, 0, 1, 2)
    lax.fori_loop(7, 11, prepare, 0)
    first_wait(0, 5, 6)
    first_start(0, 7)
    lax.fori_loop(11, blocks, prepare, 0)
    first_wait(0, 3, 4, 7)
    pick(0, 0)
    second_start(0, 0, 1, 2)

    def step(t, carry):
        @pl.when(t == 1)
        def _():
            first_wait(1, 1, 2)
            first_start(1, 5, 6)
            first_wait(1, 0)
            first_start(1, 3, 4)

        @pl.when(t == 3)
        def _():
            first_wait(1, 5, 6)
            first_start(1, 7)

        @pl.when(t + 1 < units)
        def _():
            pick(0, t + 1)

        @pl.when(t + 1 == units)
        def _():
            first_wait(1, 3, 4, 7)

        @pl.when((t + 1 >= units) & (t + 1 < steps))
        def _():
            pick(1, t + 1 - units)

        @pl.when(t + 1 < steps)
        def _():
            second_start(t + 1, 0, 1, 2)

        @pl.when(t < steps)
        def _():
            second_wait(t, 1, 2)
            second_start(t, 5, 6)
            second_wait(t, 0)
            second_start(t, 3, 4)

        @pl.when((t >= 1) & (t < steps + 1))
        def _():
            second_wait(t - 1, 5, 6)
            second_start(t - 1, 7)

        @pl.when((t >= 2) & (t < steps + 2))
        def _():
            second_wait(t - 2, 3, 4, 7)
            second_start(t - 2, 8)

        @pl.when((t >= 3) & (t < units + 3))
        def _():
            second_wait(t - 3, 8)
            multiply(0, t - 3)

        @pl.when(t >= units + 3)
        def _():
            second_wait(t - 3, 8)
            multiply(1, t - 3 - units)

        return carry

    lax.fori_loop(0, steps + 3, step, 0)
    store(units - 2).wait()
    store(units - 1).wait()
    for h in range(2):
        for kind, (ref, to) in enumerate(first_out(h)):
            first(h, kind, ref, to).wait_send()

    def finish(t, carry):
        for kind, (ref, to) in enumerate(second_out(t)):
            second(t, kind, ref, to).wait_send()
        return carry

    lax.fori_loop(0, steps, finish, 0)


def run_gather_project(size, order, idx, tokens, weight, gain):
    row_count = lax.axis_size("row")
    groups = tokens.shape[0]
    count = size // UNITS
    width = weight.shape[1] * weight.shape[2]
    depth = weight.shape[0]
    return pl.pallas_call(
        functools.partial(gather_project, UNITS),
        out_shape=jax.ShapeDtypeStruct((size,) + weight.shape[1:], jnp.bfloat16),
        in_specs=[
            pl.BlockSpec(memory_space=pltpu.SMEM),
            pl.BlockSpec(memory_space=pl.ANY),
            pl.BlockSpec(memory_space=pl.ANY),
            pl.BlockSpec(memory_space=VMEM),
        ],
        out_specs=pl.BlockSpec(memory_space=pl.ANY),
        scratch_shapes=[
            VMEM((row_count * groups, GROUP, 128), jnp.bfloat16),
            VMEM((row_count * groups, GROUP, 128), jnp.bfloat16),
            VMEM((2, 2, 8, size, 128), jnp.bfloat16),
            VMEM((2, depth // 2, width), jnp.bfloat16),
            VMEM((size, width), jnp.bfloat16),
            VMEM((2, 256) + weight.shape[1:], jnp.bfloat16),
            VMEM((2, count) + weight.shape[1:], jnp.bfloat16),
            pltpu.SemaphoreType.DMA((4,)),
            pltpu.SemaphoreType.DMA((2, 8)),
            pltpu.SemaphoreType.DMA((2, 8)),
            pltpu.SemaphoreType.DMA((2 * UNITS, 9)),
            pltpu.SemaphoreType.DMA((2 * UNITS, 9)),
            pltpu.SemaphoreType.DMA((2,)),
        ],
        compiler_params=pltpu.CompilerParams(
            collective_id=order, has_side_effects=True, vmem_limit_bytes=60 * 2**20),
        name=f"gather_project_{size}",
    )(idx, tokens, weight, gain)


def lay_out(begin, length, kv, out, held, zeros, load_sem, sem, zero_sem):
    samples, plen = out.shape[0], out.shape[1]
    pieces = load_sem.shape[0]
    per_piece = kv.shape[0] // pieces

    def load(i):
        rows = pl.ds(i * per_piece, per_piece)
        return pltpu.make_async_copy(kv.at[rows], held.at[rows], load_sem.at[i])

    for i in range(pieces):
        load(i).start()
    zeros[...] = jnp.zeros_like(zeros)

    def rows(s):
        n = length[s]
        return pltpu.make_async_copy(held.at[pl.ds(begin[s], n)], out.at[s, pl.ds(0, n)], sem.at[s])

    def rest(s):
        n = length[s]
        return pltpu.make_async_copy(zeros.at[pl.ds(0, plen - n)], out.at[s, pl.ds(n, plen - n)], zero_sem.at[s])

    for s in range(samples):
        @pl.when(length[s] < plen)
        def _():
            rest(s).start()

    for i in range(pieces):
        load(i).wait()
    for s in range(samples):
        rows(s).start()
    for s in range(samples):
        rows(s).wait()

        @pl.when(length[s] < plen)
        def _():
            rest(s).wait()


def run_lay_out(begin, length, kv):
    samples = begin.shape[0]
    return pl.pallas_call(
        lay_out,
        out_shape=jax.ShapeDtypeStruct((samples, PLEN) + kv.shape[1:], kv.dtype),
        in_specs=[
            pl.BlockSpec(memory_space=pltpu.SMEM),
            pl.BlockSpec(memory_space=pltpu.SMEM),
            pl.BlockSpec(memory_space=pl.ANY),
        ],
        out_specs=pl.BlockSpec(memory_space=pl.ANY),
        scratch_shapes=[
            VMEM(kv.shape, kv.dtype),
            VMEM((PLEN,) + kv.shape[1:], kv.dtype),
            pltpu.SemaphoreType.DMA((4,)),
            pltpu.SemaphoreType.DMA((samples,)),
            pltpu.SemaphoreType.DMA((samples,)),
        ],
        name="lay_out",
    )(begin, length, kv)


def any_size(tokens, norm_gain, projection, wanted, first_token, passage_len):
    rows_here, columns = tokens.shape
    model_width = columns * lax.axis_size("head")
    pair_count, inner_dev = (projection.shape[1], projection.shape[2])
    flat_weight = projection.reshape(model_width, pair_count * inner_dev)
    gathered = lax.all_gather(tokens, "head", axis=1, tiled=True)
    widened = gathered.astype(jnp.float32)
    inverse = lax.rsqrt(jnp.mean(widened * widened, axis=1, keepdims=True) + epsilon)
    normed = (widened * inverse * norm_gain[None, :]).astype(jnp.bfloat16)
    projected = jnp.dot(normed, flat_weight, preferred_element_type=jnp.float32)
    kv_rows = projected.astype(jnp.bfloat16).reshape(rows_here, pair_count, inner_dev)
    everything = lax.all_gather(kv_rows, "row", axis=0, tiled=True)
    positions = jnp.arange(PLEN, dtype=jnp.int32)
    target = first_token[:, None] + positions[None, :]
    filled = positions[None, :] < passage_len[:, None]
    picked = jnp.take(everything, jnp.clip(target, 0, everything.shape[0] - 1), axis=0)
    return jnp.where(filled[:, :, None, None], picked, jnp.zeros((), jnp.bfloat16))


def shards(tokens, norm_gain, projection, lengths, sample_passage):
    rows_here, columns = tokens.shape
    row_count = lax.axis_size("row")
    row_index = lax.axis_index("row")
    samp_here = sample_passage.shape[0] // row_count
    block_count, per_block = lengths.shape
    passages = block_count * per_block

    starts = jnp.cumsum(lengths, axis=1) - lengths
    block_base = (jnp.arange(block_count, dtype=jnp.int32) * rows_here)[:, None]
    offset = (starts + block_base).reshape(-1)
    length = lengths.reshape(-1)
    group_first = offset // GROUP
    group_last = (offset + length - 1) // GROUP
    order = jnp.arange(passages, dtype=jnp.int32)
    wanted = sample_passage.reshape(row_count, samp_here)
    flags = jnp.any(wanted[:, :, None] == order[None, None, :], axis=1)
    before = order[None, :] < order[:, None]
    covered = jnp.max(jnp.where(flags[:, None, :] & before[None], group_last[None, None, :], -1), axis=2)
    begin = jnp.maximum(group_first[None, :], covered + 1)
    number = jnp.where(flags, jnp.maximum(group_last[None, :] - begin + 1, 0), 0)
    ahead = jnp.sum(jnp.where(before[None], number[:, None, :], 0), axis=2)
    most = jnp.max(jnp.sum(number, axis=1)) * GROUP

    pick_row = jnp.arange(row_count, dtype=jnp.int32) == row_index

    def own(table):
        return jnp.sum(jnp.where(pick_row[:, None], table, 0), axis=0)

    number_own, ahead_own, begin_own, covered_own, wanted_own = (
        own(number), own(ahead), own(begin), own(covered), own(wanted))
    slot = jnp.arange(SIZES[-1] // GROUP, dtype=jnp.int32)[:, None]
    here = (slot >= ahead_own[None, :]) & (slot < (ahead_own + number_own)[None, :])
    idx = jnp.sum(jnp.where(here, begin_own[None, :] + slot - ahead_own[None, :], 0), axis=1)
    place = (ahead_own - (covered_own >= group_first).astype(jnp.int32)) * GROUP + offset % GROUP
    match = wanted_own[:, None] == order[None, :]

    def of_sample(table):
        return jnp.sum(jnp.where(match, table[None, :], 0), axis=1)

    first_row, first_token, passage_len = of_sample(place), of_sample(offset), of_sample(length)

    def sized(number_of, size):
        def branch():
            kv = run_gather_project(size, number_of, idx[:size // GROUP], tokens.reshape(-1, GROUP, columns), projection,
                                    norm_gain.reshape(-1, 128))
            return run_lay_out(first_row, passage_len, kv)

        return branch

    def rest():
        return any_size(tokens, norm_gain, projection, wanted_own, first_token, passage_len)

    branches = [sized(i, size) for i, size in enumerate(SIZES)] + [rest]
    tier = jnp.sum(jnp.array(SIZES, jnp.int32) < most)
    return lax.switch(tier, branches)


def solution(mesh):
    in_specs = (P("row", "head"), P(), P(None, None, "head"), P(), P())
    out_specs = P("row", None, None, "head")
    return jax.shard_map(shards, mesh=mesh, in_specs=in_specs, out_specs=out_specs, check_vma=False)
```

```python
import functools

import jax
import jax.numpy as jnp
from jax import lax
from jax.experimental import pallas as pl
from jax.experimental.pallas import tpu as pltpu
from jax.sharding import PartitionSpec as P

PLEN = 256
epsilon = 1e-06
MESH = pl.DeviceIdType.MESH
VMEM = pltpu.VMEM
UNITS = 8
GROUP = 8
SIZES = (2560, 2816, 3072, 3328)


def gather_project(units, idx, tokens, weight, gain, kv, raw_a, raw_b, spread, matrix, partial, stage, packed,
                   pool, load_sem, send1, recv1, send2, recv2, send3, recv3, keep_sem, out_sem):
    raws = (raw_a, raw_b)
    rows_all = spread.shape[3]
    count = rows_all // units
    half_count = count // 2
    groups = tokens.shape[0]
    steps = 2 * units
    row = lax.axis_index("row")
    head = lax.axis_index("head")
    y_lo, z = row // 4, row % 4
    core = head % 2
    yx = head // 2
    y_hi, x = yx // 4, yx % 4
    y_other = (1 - y_lo) * 4
    z_up, z_down, z_far = (z + 1) % 4, (z + 3) % 4, (z + 2) % 4
    x_up, x_down, x_far = (x + 1) % 4, (x + 3) % 4, (x + 2) % 4
    h_mine, h_other = y_hi * 4, (1 - y_hi) * 4

    to_y = (y_other + z, head)
    to_zu = (y_lo * 4 + z_up, head)
    to_zd = (y_lo * 4 + z_down, head)
    to_yy = (row, (h_other + x) * 2 + core)
    to_xu = (row, (h_mine + x_up) * 2 + core)
    to_xd = (row, (h_mine + x_down) * 2 + core)
    to_sib = (row, yx * 2 + 1 - core)

    barrier = pltpu.get_barrier_semaphore()
    for peer in (to_y, to_zu, to_zd, to_yy, to_xu, to_xd, to_sib):
        pl.semaphore_signal(barrier, inc=1, device_id=peer, device_id_type=MESH)

    def load(h):
        return pltpu.make_async_copy(tokens.at[:, :, pl.ds(h * 128, 128)], raws[h].at[pl.ds(row * groups, groups)],
                                     load_sem.at[h])

    load(0).start()
    load(1).start()

    def block(h, r, part=None):
        if part is None:
            return raws[h].at[pl.ds(r * groups, groups)]
        return raws[h].at[pl.ds(r * groups + part * (groups // 2), groups // 2)]

    def first(h, kind, ref, to):
        return pltpu.make_async_remote_copy(src_ref=ref, dst_ref=ref, send_sem=send1.at[h, kind],
                                            recv_sem=recv1.at[h, kind], device_id=to, device_id_type=MESH)

    def first_out(h):
        mine = block(h, row)
        other = block(h, y_other + z)
        return [
            (mine, to_y), (mine, to_zu), (mine, to_zd), (other, to_zu), (other, to_zd),
            (block(h, y_lo * 4 + z_down, 0), to_zu), (block(h, y_lo * 4 + z_up, 1), to_zd),
        ] + ([(block(h, y_lo * 4 + z_far), to_y)] if h == 0 else [
            (block(h, y_other + z_down, 0), to_zu), (block(h, y_other + z_up, 1), to_zd)])

    def first_in(h):
        return [
            block(h, y_other + z), block(h, y_lo * 4 + z_down), block(h, y_lo * 4 + z_up), block(h, y_other + z_down),
            block(h, y_other + z_up), block(h, y_lo * 4 + z_far, 0), block(h, y_lo * 4 + z_far, 1),
        ] + ([block(h, y_other + z_far)] if h == 0 else [
            block(h, y_other + z_far, 0), block(h, y_other + z_far, 1)])

    def first_start(h, *kinds):
        out = first_out(h)
        for kind in kinds:
            first(h, kind, *out[kind]).start()

    def first_wait(h, *kinds):
        got = first_in(h)
        for kind in kinds:
            first(h, kind, got[kind], to_y).wait_recv()

    blocks = weight.shape[0] // 256

    def fetch(i):
        return pltpu.make_async_copy(weight.at[pl.ds(i * 256, 256)], stage.at[i % 2], load_sem.at[2 + i % 2])

    fetch(0).start()

    def prepare(i, carry):
        @pl.when(i + 1 < blocks)
        def _():
            fetch(i + 1).start()

        fetch(i).wait()
        block_now = stage[i % 2]
        for h in range(2):
            scale = jnp.broadcast_to(gain[pl.ds(2 * i + h, 1), :], (128, 128)).T
            scale = jnp.concatenate([scale, scale], axis=1)
            for c in range(4):
                part = block_now[h * 128:h * 128 + 128, c, :].astype(jnp.float32) * scale
                matrix[h, pl.ds(pl.multiple_of(i * 128, 128), 128), c * 256:c * 256 + 256] = part.astype(jnp.bfloat16)
        return carry

    def slab(h, c, p, u, part=None):
        if part is None:
            return spread.at[h, c, p, pl.ds(pl.multiple_of(u * count, 32), count)]
        return spread.at[h, c, p, pl.ds(pl.multiple_of(u * count + part * half_count, 16), half_count)]

    def second(t, kind, ref, to):
        return pltpu.make_async_remote_copy(src_ref=ref, dst_ref=ref, send_sem=send2.at[t, kind],
                                            recv_sem=recv2.at[t, kind], device_id=to, device_id_type=MESH)

    def both(h, c, u):
        return spread.at[h, c, :, pl.ds(pl.multiple_of(u * count, 32), count)]

    def second_out(t):
        h, u = t // units, t % units
        mine = slab(h, core, yx, u)
        other = slab(h, core, h_other + x, u)
        return [
            (mine, to_yy), (mine, to_xu), (mine, to_xd), (other, to_xu), (other, to_xd),
            (slab(h, core, h_mine + x_down, u, 0), to_xu), (slab(h, core, h_mine + x_up, u, 1), to_xd),
            (slab(h, core, h_mine + x_far, u), to_yy), (both(h, core, u), to_sib),
        ]

    def second_in(t):
        h, u = t // units, t % units
        return [
            slab(h, core, h_other + x, u), slab(h, core, h_mine + x_down, u), slab(h, core, h_mine + x_up, u),
            slab(h, core, h_other + x_down, u), slab(h, core, h_other + x_up, u), slab(h, core, h_mine + x_far, u, 0),
            slab(h, core, h_mine + x_far, u, 1), slab(h, core, h_other + x_far, u), both(h, 1 - core, u),
        ]

    def second_start(t, *kinds):
        out = second_out(t)
        for kind in kinds:
            second(t, kind, *out[kind]).start()

    def second_wait(t, *kinds):
        got = second_in(t)
        for kind in kinds:
            second(t, kind, got[kind], to_yy).wait_recv()

    def pick(h, u):
        def two(k, carry):
            g = u * (count // GROUP) + 2 * k
            pair = jnp.concatenate([raws[h][idx[0, g]], raws[h][idx[0, g + 1]]], axis=0)
            spread[h, core, yx, pl.ds(pl.multiple_of(u * count + k * 16, 16), 16), :] = pair
            return carry

        lax.fori_loop(0, count // 16, two, 0, unroll=2)

    pool_rows = pool.shape[0] * half_count

    def store(u):
        return pltpu.make_async_copy(packed.at[u % 2], kv.at[pl.ds(pool_rows + u * count, count)], out_sem.at[u % 2])

    def share(r, part=None):
        if part is None:
            return pool.at[r]
        return pool.at[r, pl.ds(part * (half_count // 2), half_count // 2)]

    def third(kind, ref, to):
        return pltpu.make_async_remote_copy(src_ref=ref, dst_ref=ref, send_sem=send3.at[kind], recv_sem=recv3.at[kind],
                                            device_id=to, device_id_type=MESH)

    third_out = [
        (share(row), to_y), (share(row), to_zu), (share(row), to_zd), (share(y_other + z), to_zu),
        (share(y_other + z), to_zd), (share(y_lo * 4 + z_down, 0), to_zu), (share(y_lo * 4 + z_up, 1), to_zd),
        (share(y_other + z_down, 0), to_zu), (share(y_other + z_up, 1), to_zd),
    ]
    third_in = [
        share(y_other + z), share(y_lo * 4 + z_down), share(y_lo * 4 + z_up), share(y_other + z_down),
        share(y_other + z_up), share(y_lo * 4 + z_far, 0), share(y_lo * 4 + z_far, 1), share(y_other + z_far, 0),
        share(y_other + z_far, 1),
    ]

    def third_start(*kinds):
        for kind in kinds:
            third(kind, *third_out[kind]).start()

    def third_wait(*kinds):
        for kind in kinds:
            third(kind, third_in[kind], to_y).wait_recv()

    def multiply(h, u):
        if h == 1:
            @pl.when(u >= 2)
            def _():
                store(u - 2).wait()

        def piece(k, carry):
            rows = pl.ds(pl.multiple_of(u * count + k * half_count, 16), half_count)
            parts = [spread[h, j % 2, j // 2, rows, :] for j in range(16)]
            left = jnp.concatenate(parts, axis=1)
            if h == 0:
                for c in range(4):
                    cols = slice(c * 256, c * 256 + 256)
                    value = jnp.dot(left, matrix[0, :, cols], preferred_element_type=jnp.float32)
                    partial[rows, cols] = value.astype(jnp.bfloat16)
                return carry
            total = jnp.zeros((half_count, 128), jnp.float32)
            for part in parts + [spread[0, j % 2, j // 2, rows, :] for j in range(16)]:
                wide = part.astype(jnp.float32)
                total = total + wide * wide
            inverse = lax.rsqrt(jnp.sum(total, axis=1, keepdims=True) / (32.0 * 128.0) + epsilon)
            outs = []
            for c in range(4):
                cols = slice(c * 256, c * 256 + 256)
                value = jnp.dot(left, matrix[1, :, cols], preferred_element_type=jnp.float32)
                value = value + partial[rows, cols].astype(jnp.float32)
                outs.append((value * inverse).astype(jnp.bfloat16))
            packed[u % 2, pl.ds(pl.multiple_of(k * half_count, 16), half_count)] = jnp.stack(outs, axis=1)

            @pl.when(2 * u + k == 0)
            def _():
                pool[row] = packed[0, 0:half_count]

            return carry

        lax.fori_loop(0, 2, piece, 0)
        if h == 1:
            store(u).start()

    load(0).wait()
    pl.semaphore_wait(barrier, 7)
    first_start(0, 0, 1, 2)
    lax.fori_loop(0, 7, prepare, 0)
    first_wait(0, 1, 2)
    first_start(0, 5, 6)
    first_wait(0, 0)
    first_start(0, 3, 4)
    load(1).wait()
    first_start(1, 0, 1, 2)
    lax.fori_loop(7, 11, prepare, 0)
    first_wait(0, 5, 6)
    first_start(0, 7)
    lax.fori_loop(11, blocks, prepare, 0)
    first_wait(0, 3, 4, 7)
    pick(0, 0)
    second_start(0, 0, 1, 2)

    def first_sent(h):
        for kind, (ref, to) in enumerate(first_out(h)):
            first(h, kind, ref, to).wait_send()

    def second_sent(t):
        for kind, (ref, to) in enumerate(second_out(t)):
            second(t, kind, ref, to).wait_send()

    def keep(r):
        return pltpu.make_async_copy(pool.at[r], kv.at[pl.ds(r * half_count, half_count)], keep_sem.at[r])

    def step(t, carry):
        @pl.when(t == steps)
        def _():
            third_wait(3, 4)
            third_start(7, 8)
            third_wait(5, 6)
            for y in (0, 4):
                keep(y + z).start()
                keep(y + z_up).start()
                keep(y + z_down).start()
            keep(y_lo * 4 + z_far).start()

        @pl.when(t == 1)
        def _():
            first_wait(1, 1, 2)
            first_start(1, 5, 6)
            first_wait(1, 0)
            first_start(1, 3, 4)

        @pl.when(t == 3)
        def _():
            first_wait(1, 3, 4)
            first_start(1, 7, 8)
            first_sent(0)

        @pl.when(t + 1 < units)
        def _():
            pick(0, t + 1)

        @pl.when(t + 1 == units)
        def _():
            first_wait(1, 5, 6, 7, 8)

        @pl.when((t + 1 >= units) & (t + 1 < steps))
        def _():
            pick(1, t + 1 - units)

        @pl.when(t + 1 < steps)
        def _():
            second_start(t + 1, 0, 1, 2)

        @pl.when(t == units)
        def _():
            first_sent(1)

        @pl.when(t < steps)
        def _():
            second_wait(t, 1, 2)
            second_start(t, 5, 6)
            second_wait(t, 0)
            second_start(t, 3, 4)

        @pl.when((t >= 1) & (t < steps + 1))
        def _():
            second_wait(t - 1, 5, 6)
            second_start(t - 1, 7)

        @pl.when((t >= 2) & (t < steps + 2))
        def _():
            second_wait(t - 2, 3, 4, 7)
            second_start(t - 2, 8)

        @pl.when((t >= 3) & (t < units + 3))
        def _():
            second_wait(t - 3, 8)
            multiply(0, t - 3)

        @pl.when(t >= units + 3)
        def _():
            second_wait(t - 3, 8)
            multiply(1, t - 3 - units)

        @pl.when(t == units + 3)
        def _():
            third_start(0, 1, 2)

        @pl.when(t == units + 5)
        def _():
            third_wait(1, 2)
            third_start(5, 6)
            third_wait(0)
            third_start(3, 4)


        @pl.when(t >= 5)
        def _():
            second_sent(t - 5)

        return carry

    lax.fori_loop(0, steps + 3, step, 0)
    third_wait(7, 8)
    keep(y_other + z_far).start()
    for r in range(pool.shape[0]):
        keep(r).wait()
    for kind, (ref, to) in enumerate(third_out):
        third(kind, ref, to).wait_send()
    store(units - 2).wait()
    store(units - 1).wait()
    second_sent(steps - 2)
    second_sent(steps - 1)


def run_gather_project(size, order, idx, tokens, weight, gain):
    row_count = lax.axis_size("row")
    groups = tokens.shape[0]
    count = size // UNITS
    width = weight.shape[1] * weight.shape[2]
    depth = weight.shape[0]
    return pl.pallas_call(
        functools.partial(gather_project, UNITS),
        out_shape=jax.ShapeDtypeStruct((size + row_count * count // 2,) + weight.shape[1:], jnp.bfloat16),
        in_specs=[
            pl.BlockSpec(memory_space=pltpu.SMEM),
            pl.BlockSpec(memory_space=pl.ANY),
            pl.BlockSpec(memory_space=pl.ANY),
            pl.BlockSpec(memory_space=VMEM),
        ],
        out_specs=pl.BlockSpec(memory_space=pl.ANY),
        scratch_shapes=[
            VMEM((row_count * groups, GROUP, 128), jnp.bfloat16),
            VMEM((row_count * groups, GROUP, 128), jnp.bfloat16),
            VMEM((2, 2, 8, size, 128), jnp.bfloat16),
            VMEM((2, depth // 2, width), jnp.bfloat16),
            VMEM((size, width), jnp.bfloat16),
            VMEM((2, 256) + weight.shape[1:], jnp.bfloat16),
            VMEM((2, count) + weight.shape[1:], jnp.bfloat16),
            VMEM((row_count, count // 2) + weight.shape[1:], jnp.bfloat16),
            pltpu.SemaphoreType.DMA((4,)),
            pltpu.SemaphoreType.DMA((2, 9)),
            pltpu.SemaphoreType.DMA((2, 9)),
            pltpu.SemaphoreType.DMA((2 * UNITS, 9)),
            pltpu.SemaphoreType.DMA((2 * UNITS, 9)),
            pltpu.SemaphoreType.DMA((9,)),
            pltpu.SemaphoreType.DMA((9,)),
            pltpu.SemaphoreType.DMA((row_count,)),
            pltpu.SemaphoreType.DMA((2,)),
        ],
        compiler_params=pltpu.CompilerParams(
            collective_id=order, has_side_effects=True, vmem_limit_bytes=60 * 2**20),
        name=f"gather_project_{size}",
    )(idx, tokens, weight, gain)


def lay_out(table, kv, out, held, zeros, load_sem, sem, zero_sem):
    samples, plen = out.shape[0], out.shape[1]
    pieces = load_sem.shape[0]
    per_piece = kv.shape[0] // pieces

    def load(i):
        rows = pl.ds(i * per_piece, per_piece)
        return pltpu.make_async_copy(kv.at[rows], held.at[rows], load_sem.at[i])

    for i in range(pieces):
        load(i).start()
    zeros[...] = jnp.zeros_like(zeros)

    def rows(s):
        n = table[1, s]
        return pltpu.make_async_copy(held.at[pl.ds(table[0, s], n)], out.at[s, pl.ds(0, n)], sem.at[s])

    def rest(s):
        n = table[1, s]
        return pltpu.make_async_copy(zeros.at[pl.ds(0, plen - n)], out.at[s, pl.ds(n, plen - n)], zero_sem.at[s])

    for s in range(samples):
        @pl.when(table[1, s] < plen)
        def _():
            rest(s).start()

    for i in range(pieces):
        load(i).wait()
    for s in range(samples):
        rows(s).start()
    for s in range(samples):
        rows(s).wait()

        @pl.when(table[1, s] < plen)
        def _():
            rest(s).wait()


def run_lay_out(table, samples, kv):
    return pl.pallas_call(
        lay_out,
        out_shape=jax.ShapeDtypeStruct((samples, PLEN) + kv.shape[1:], kv.dtype),
        in_specs=[
            pl.BlockSpec(memory_space=pltpu.SMEM),
            pl.BlockSpec(memory_space=pl.ANY),
        ],
        out_specs=pl.BlockSpec(memory_space=pl.ANY),
        scratch_shapes=[
            VMEM(kv.shape, kv.dtype),
            VMEM((PLEN,) + kv.shape[1:], kv.dtype),
            pltpu.SemaphoreType.DMA((4,)),
            pltpu.SemaphoreType.DMA((samples,)),
            pltpu.SemaphoreType.DMA((samples,)),
        ],
        name="lay_out",
    )(table, kv)


def any_size(tokens, norm_gain, projection, first_token, passage_len):
    rows_here, columns = tokens.shape
    model_width = columns * lax.axis_size("head")
    pair_count, inner_dev = (projection.shape[1], projection.shape[2])
    flat_weight = projection.reshape(model_width, pair_count * inner_dev)
    gathered = lax.all_gather(tokens, "head", axis=1, tiled=True)
    widened = gathered.astype(jnp.float32)
    inverse = lax.rsqrt(jnp.mean(widened * widened, axis=1, keepdims=True) + epsilon)
    normed = (widened * inverse * norm_gain[None, :]).astype(jnp.bfloat16)
    projected = jnp.dot(normed, flat_weight, preferred_element_type=jnp.float32)
    kv_rows = projected.astype(jnp.bfloat16).reshape(rows_here, pair_count, inner_dev)
    everything = lax.all_gather(kv_rows, "row", axis=0, tiled=True)
    positions = jnp.arange(PLEN, dtype=jnp.int32)
    target = first_token[:, None] + positions[None, :]
    filled = positions[None, :] < passage_len[:, None]
    picked = jnp.take(everything, jnp.clip(target, 0, everything.shape[0] - 1), axis=0)
    return jnp.where(filled[:, :, None, None], picked, jnp.zeros((), jnp.bfloat16))


def plan(row_count, lengths, sample_passage, idx, table, match):
    blocks, per_block = lengths.shape
    samples = sample_passage.shape[1]
    here = samples // row_count
    passages = blocks * per_block
    f32 = jnp.float32
    row = lax.axis_index("row")
    mine = row.astype(f32)

    def iota(shape, axis):
        return lax.broadcasted_iota(jnp.int32, shape, axis)

    square = (128, 128)
    diagonal = iota(square, 0) == iota(square, 1)
    before = iota(square, 1) < iota(square, 0)
    lane = iota((1, 128), 1)

    def down(value):
        return jnp.sum(jnp.where(diagonal, value, 0.0), axis=1, keepdims=True)

    def along(value):
        return jnp.sum(jnp.where(diagonal, value, 0.0), axis=0, keepdims=True)

    length = jnp.zeros((1, 128), f32)
    spot = iota((per_block, 128), 1) - iota((per_block, 128), 0)
    for b in range(blocks):
        column = jnp.sum(jnp.where(iota((per_block, per_block), 0) == iota((per_block, per_block), 1),
                                   lengths[b:b + 1, :].astype(f32), 0.0), axis=1, keepdims=True)
        length = length + jnp.sum(jnp.where(spot == b * per_block, column, 0.0), axis=0, keepdims=True)
    offset_d = jnp.sum(jnp.where(before, length, 0.0), axis=1, keepdims=True)
    offset = along(offset_d)
    begin = jnp.floor(offset / GROUP)
    groups = jnp.where(lane < passages, jnp.floor((offset + length - 1.0) / GROUP) - begin + 1.0, 0.0)
    begin_d, groups_d = down(begin), down(groups)

    asked = sample_passage[...].astype(f32)
    same = iota((samples, samples), 0) == iota((samples, samples), 1)
    asked_d = jnp.sum(jnp.where(same, asked, 0.0), axis=1, keepdims=True)
    match[...] = (asked_d == iota((samples, 128), 1).astype(f32)).astype(f32)
    flags = jnp.concatenate(
        [jnp.max(match[r * here:(r + 1) * here, :], axis=0, keepdims=True) for r in range(row_count)], axis=0)
    load = jnp.sum(flags * groups, axis=1, keepdims=True)
    ratio = load / jnp.max(load)
    weight = (ratio * ratio) * (ratio * ratio)
    score = jnp.sum(flags * weight, axis=0, keepdims=True)
    score_d = down(score)
    above = (score > score_d) | ((score == score_d) & before)
    pool_ahead_d = jnp.sum(jnp.where(above, groups, 0.0), axis=1, keepdims=True)
    pool_ahead = along(pool_ahead_d)

    tier = jnp.full((1, 1), float(len(SIZES)), f32)
    share = jnp.zeros((1, 1), f32)
    for number in reversed(range(len(SIZES))):
        part = SIZES[number] // (2 * UNITS * GROUP)
        alone = jnp.where(pool_ahead + groups <= float(part * row_count), 0.0, flags * groups)
        most = jnp.max(jnp.sum(alone, axis=1, keepdims=True), axis=0, keepdims=True)
        fits = most + part <= float(SIZES[number] // GROUP)
        tier = jnp.where(fits, float(number), tier)
        share = jnp.where(fits, float(part), share)

    pooled = pool_ahead + groups <= share * row_count
    pooled_d = pool_ahead_d + groups_d <= share * row_count
    flag_own = jnp.sum(jnp.where(iota((row_count, 128), 0) == row, flags, 0.0), axis=0, keepdims=True)
    number = jnp.where(pooled, 0.0, flag_own * groups)
    number_d = down(number)
    ahead_d = share + jnp.sum(jnp.where(before, number, 0.0), axis=1, keepdims=True)
    slots = idx.shape[1]
    slot = iota((1, slots), 1).astype(f32)
    pool_slot = jnp.where(slot < share, slot + mine * share, -1.0)
    alone = (slot >= ahead_d) & (slot < ahead_d + number_d)
    common = pooled_d & (pool_slot >= pool_ahead_d) & (pool_slot < pool_ahead_d + groups_d)
    value = jnp.where(alone, begin_d + (slot - ahead_d), 0.0) + jnp.where(common, begin_d + (pool_slot - pool_ahead_d), 0.0)
    idx[...] = jnp.sum(value, axis=0, keepdims=True).astype(jnp.int32)

    place = jnp.where(pooled, pool_ahead, share * row_count + along(ahead_d)) * GROUP + (offset - begin * GROUP)
    own_match = match[pl.ds(pl.multiple_of(row * here, 8), here), :]
    lined = iota((here, 128), 0) == iota((here, 128), 1)

    def of_sample(value):
        found = jnp.sum(own_match * value, axis=1, keepdims=True)
        return jnp.sum(jnp.where(lined, found, 0.0), axis=0, keepdims=True)

    rows = [of_sample(place), of_sample(length), of_sample(offset), jnp.broadcast_to(tier, (1, 128))]
    table[...] = jnp.concatenate(rows + rows, axis=0).astype(jnp.int32)


def run_plan(lengths, sample_passage, row_count):
    return pl.pallas_call(
        functools.partial(plan, row_count),
        out_shape=(jax.ShapeDtypeStruct((1, 512), jnp.int32), jax.ShapeDtypeStruct((8, 128), jnp.int32)),
        in_specs=[pl.BlockSpec(memory_space=VMEM)] * 2,
        out_specs=(pl.BlockSpec(memory_space=VMEM), pl.BlockSpec(memory_space=VMEM)),
        scratch_shapes=[VMEM((sample_passage.shape[1], 128), jnp.float32)],
        compiler_params=pltpu.CompilerParams(vmem_limit_bytes=8 * 2**20),
        name="plan",
    )(lengths, sample_passage)


def shards(tokens, norm_gain, projection, lengths, sample_passage):
    columns = tokens.shape[1]
    row_count = lax.axis_size("row")
    samp_here = sample_passage.shape[0] // row_count
    idx, table = run_plan(lengths, sample_passage.reshape(1, -1), row_count)

    def sized(number_of, size):
        def branch():
            kv = run_gather_project(size, number_of, idx, tokens.reshape(-1, GROUP, columns), projection,
                                    norm_gain.reshape(-1, 128))
            return run_lay_out(table, samp_here, kv)

        return branch

    def rest():
        return any_size(tokens, norm_gain, projection, table[2, :samp_here], table[1, :samp_here])

    branches = [sized(i, size) for i, size in enumerate(SIZES)] + [rest]
    return lax.switch(table[3, 0], branches)


def solution(mesh):
    in_specs = (P("row", "head"), P(), P(None, None, "head"), P(), P())
    out_specs = P("row", None, None, "head")
    return jax.shard_map(shards, mesh=mesh, in_specs=in_specs, out_specs=out_specs, check_vma=False)
```

```python
import functools

import jax
import jax.numpy as jnp
from jax import lax
from jax.experimental import pallas as pl
from jax.experimental.pallas import tpu as pltpu
from jax.sharding import PartitionSpec as P

PLEN = 256
epsilon = 1e-06
MESH = pl.DeviceIdType.MESH
VMEM = pltpu.VMEM
UNITS = 8
GROUP = 8
SIZES = (2560, 2816, 3072, 3328)


def gather_project(units, idx, tokens, weight, gain, kv, raw_a, raw_b, spread, matrix, partial, stage, packed,
                   pool, load_sem, send1, recv1, send2, recv2, send3, recv3, keep_sem, out_sem):
    raws = (raw_a, raw_b)
    rows_all = spread.shape[3]
    count = rows_all // units
    half_count = count // 2
    groups = tokens.shape[0]
    steps = 2 * units
    early = units - 2
    row = lax.axis_index("row")
    head = lax.axis_index("head")
    y_lo, z = row // 4, row % 4
    core = head % 2
    yx = head // 2
    y_hi, x = yx // 4, yx % 4
    y_other = (1 - y_lo) * 4
    z_up, z_down, z_far = (z + 1) % 4, (z + 3) % 4, (z + 2) % 4
    x_up, x_down, x_far = (x + 1) % 4, (x + 3) % 4, (x + 2) % 4
    h_mine, h_other = y_hi * 4, (1 - y_hi) * 4

    to_y = (y_other + z, head)
    to_zu = (y_lo * 4 + z_up, head)
    to_zd = (y_lo * 4 + z_down, head)
    to_yy = (row, (h_other + x) * 2 + core)
    to_xu = (row, (h_mine + x_up) * 2 + core)
    to_xd = (row, (h_mine + x_down) * 2 + core)
    to_sib = (row, yx * 2 + 1 - core)

    barrier = pltpu.get_barrier_semaphore()
    for peer in (to_y, to_zu, to_zd, to_yy, to_xu, to_xd, to_sib):
        pl.semaphore_signal(barrier, inc=1, device_id=peer, device_id_type=MESH)

    def load(h):
        return pltpu.make_async_copy(tokens.at[:, :, pl.ds(h * 128, 128)], raws[h].at[pl.ds(row * groups, groups)],
                                     load_sem.at[h])

    load(0).start()
    load(1).start()

    def block(h, r, part=None):
        if part is None:
            return raws[h].at[pl.ds(r * groups, groups)]
        return raws[h].at[pl.ds(r * groups + part * (groups // 2), groups // 2)]

    def first(h, kind, ref, to):
        return pltpu.make_async_remote_copy(src_ref=ref, dst_ref=ref, send_sem=send1.at[h, kind],
                                            recv_sem=recv1.at[h, kind], device_id=to, device_id_type=MESH)

    def first_out(h):
        mine = block(h, row)
        other = block(h, y_other + z)
        return [
            (mine, to_y), (mine, to_zu), (mine, to_zd), (other, to_zu), (other, to_zd),
            (block(h, y_lo * 4 + z_down, 0), to_zu), (block(h, y_lo * 4 + z_up, 1), to_zd),
        ] + ([(block(h, y_lo * 4 + z_far), to_y)] if h == 0 else [
            (block(h, y_other + z_down, 0), to_zu), (block(h, y_other + z_up, 1), to_zd)])

    def first_in(h):
        return [
            block(h, y_other + z), block(h, y_lo * 4 + z_down), block(h, y_lo * 4 + z_up), block(h, y_other + z_down),
            block(h, y_other + z_up), block(h, y_lo * 4 + z_far, 0), block(h, y_lo * 4 + z_far, 1),
        ] + ([block(h, y_other + z_far)] if h == 0 else [
            block(h, y_other + z_far, 0), block(h, y_other + z_far, 1)])

    def first_start(h, *kinds):
        out = first_out(h)
        for kind in kinds:
            first(h, kind, *out[kind]).start()

    def first_wait(h, *kinds):
        got = first_in(h)
        for kind in kinds:
            first(h, kind, got[kind], to_y).wait_recv()

    blocks = weight.shape[0] // 256

    def fetch(i):
        return pltpu.make_async_copy(weight.at[pl.ds(i * 256, 256)], stage.at[i % 2], load_sem.at[2 + i % 2])

    fetch(0).start()

    def prepare(i, carry):
        @pl.when(i + 1 < blocks)
        def _():
            fetch(i + 1).start()

        fetch(i).wait()
        block_now = stage[i % 2]
        for h in range(2):
            scale = jnp.broadcast_to(gain[pl.ds(2 * i + h, 1), :], (128, 128)).T
            scale = jnp.concatenate([scale, scale], axis=1)
            for c in range(4):
                part = block_now[h * 128:h * 128 + 128, c, :].astype(jnp.float32) * scale
                matrix[h, pl.ds(pl.multiple_of(i * 128, 128), 128), c * 256:c * 256 + 256] = part.astype(jnp.bfloat16)
        return carry

    def slab(h, c, p, u, part=None):
        if part is None:
            return spread.at[h, c, p, pl.ds(pl.multiple_of(u * count, 32), count)]
        return spread.at[h, c, p, pl.ds(pl.multiple_of(u * count + part * half_count, 16), half_count)]

    def turn(t):
        return jnp.where(t < early, t, jnp.where(t == early, units, jnp.where(t <= units, t - 1, t)))

    def second(t, kind, ref, to):
        return pltpu.make_async_remote_copy(src_ref=ref, dst_ref=ref, send_sem=send2.at[t, kind],
                                            recv_sem=recv2.at[t, kind], device_id=to, device_id_type=MESH)

    def both(h, c, u):
        return spread.at[h, c, :, pl.ds(pl.multiple_of(u * count, 32), count)]

    def second_out(t):
        now = turn(t)
        h, u = now // units, now % units
        mine = slab(h, core, yx, u)
        other = slab(h, core, h_other + x, u)
        return [
            (mine, to_yy), (mine, to_xu), (mine, to_xd), (other, to_xu), (other, to_xd),
            (slab(h, core, h_mine + x_down, u, 0), to_xu), (slab(h, core, h_mine + x_up, u, 1), to_xd),
            (slab(h, core, h_mine + x_far, u), to_yy), (both(h, core, u), to_sib),
        ]

    def second_in(t):
        now = turn(t)
        h, u = now // units, now % units
        return [
            slab(h, core, h_other + x, u), slab(h, core, h_mine + x_down, u), slab(h, core, h_mine + x_up, u),
            slab(h, core, h_other + x_down, u), slab(h, core, h_other + x_up, u), slab(h, core, h_mine + x_far, u, 0),
            slab(h, core, h_mine + x_far, u, 1), slab(h, core, h_other + x_far, u), both(h, 1 - core, u),
        ]

    def second_start(t, *kinds):
        out = second_out(t)
        for kind in kinds:
            second(t, kind, *out[kind]).start()

    def second_wait(t, *kinds):
        got = second_in(t)
        for kind in kinds:
            second(t, kind, got[kind], to_yy).wait_recv()

    def pick(h, u):
        def two(k, carry):
            g = u * (count // GROUP) + 2 * k
            pair = jnp.concatenate([raws[h][idx[0, g]], raws[h][idx[0, g + 1]]], axis=0)
            spread[h, core, yx, pl.ds(pl.multiple_of(u * count + k * 16, 16), 16), :] = pair
            return carry

        lax.fori_loop(0, count // 16, two, 0, unroll=2)

    pool_rows = pool.shape[0] * half_count

    def store(u):
        return pltpu.make_async_copy(packed.at[u % 2], kv.at[pl.ds(pool_rows + u * count, count)], out_sem.at[u % 2])

    def share(r, part=None):
        if part is None:
            return pool.at[r]
        return pool.at[r, pl.ds(part * (half_count // 2), half_count // 2)]

    def third(kind, ref, to):
        return pltpu.make_async_remote_copy(src_ref=ref, dst_ref=ref, send_sem=send3.at[kind], recv_sem=recv3.at[kind],
                                            device_id=to, device_id_type=MESH)

    third_out = [
        (share(row), to_y), (share(row), to_zu), (share(row), to_zd), (share(y_other + z), to_zu),
        (share(y_other + z), to_zd), (share(y_lo * 4 + z_down, 0), to_zu), (share(y_lo * 4 + z_up, 1), to_zd),
        (share(y_other + z_down, 0), to_zu), (share(y_other + z_up, 1), to_zd),
    ]
    third_in = [
        share(y_other + z), share(y_lo * 4 + z_down), share(y_lo * 4 + z_up), share(y_other + z_down),
        share(y_other + z_up), share(y_lo * 4 + z_far, 0), share(y_lo * 4 + z_far, 1), share(y_other + z_far, 0),
        share(y_other + z_far, 1),
    ]

    def third_start(*kinds):
        for kind in kinds:
            third(kind, *third_out[kind]).start()

    def third_wait(*kinds):
        for kind in kinds:
            third(kind, third_in[kind], to_y).wait_recv()

    def multiply(h, u):
        if h == 1:
            @pl.when(u >= 2)
            def _():
                store(u - 2).wait()

        def piece(k, carry):
            rows = pl.ds(pl.multiple_of(u * count + k * half_count, 16), half_count)
            parts = [spread[h, j % 2, j // 2, rows, :] for j in range(16)]
            left = jnp.concatenate(parts, axis=1)
            if h == 0:
                for c in range(4):
                    cols = slice(c * 256, c * 256 + 256)
                    value = jnp.dot(left, matrix[0, :, cols], preferred_element_type=jnp.float32)
                    partial[rows, cols] = value.astype(jnp.bfloat16)
                return carry
            total = jnp.zeros((half_count, 128), jnp.float32)
            for part in parts + [spread[0, j % 2, j // 2, rows, :] for j in range(16)]:
                wide = part.astype(jnp.float32)
                total = total + wide * wide
            inverse = lax.rsqrt(jnp.sum(total, axis=1, keepdims=True) / (32.0 * 128.0) + epsilon)
            outs = []
            for c in range(4):
                cols = slice(c * 256, c * 256 + 256)
                value = jnp.dot(left, matrix[1, :, cols], preferred_element_type=jnp.float32)
                value = value + partial[rows, cols].astype(jnp.float32)
                outs.append((value * inverse).astype(jnp.bfloat16))
            packed[u % 2, pl.ds(pl.multiple_of(k * half_count, 16), half_count)] = jnp.stack(outs, axis=1)

            @pl.when(2 * u + k == 0)
            def _():
                pool[row] = packed[0, 0:half_count]

            return carry

        lax.fori_loop(0, 2, piece, 0)
        if h == 1:
            store(u).start()

    load(0).wait()
    pl.semaphore_wait(barrier, 7)
    first_start(0, 0, 1, 2)
    lax.fori_loop(0, 7, prepare, 0)
    first_wait(0, 1, 2)
    first_start(0, 5, 6)
    first_wait(0, 0)
    first_start(0, 3, 4)
    load(1).wait()
    first_start(1, 0, 1, 2)
    lax.fori_loop(7, 11, prepare, 0)
    first_wait(0, 5, 6)
    first_start(0, 7)
    lax.fori_loop(11, blocks, prepare, 0)
    first_wait(0, 3, 4, 7)
    pick(0, 0)
    second_start(0, 0, 1, 2)

    def first_sent(h):
        for kind, (ref, to) in enumerate(first_out(h)):
            first(h, kind, ref, to).wait_send()

    def second_sent(t):
        for kind, (ref, to) in enumerate(second_out(t)):
            second(t, kind, ref, to).wait_send()

    def keep(r):
        return pltpu.make_async_copy(pool.at[r], kv.at[pl.ds(r * half_count, half_count)], keep_sem.at[r])

    def step(t, carry):
        @pl.when(t == steps)
        def _():
            third_wait(5, 6)
            for y in (0, 4):
                keep(y + z).start()
                keep(y + z_up).start()
                keep(y + z_down).start()
            keep(y_lo * 4 + z_far).start()

        @pl.when(t == 1)
        def _():
            first_wait(1, 1, 2)
            first_start(1, 5, 6)
            first_wait(1, 0)
            first_start(1, 3, 4)

        @pl.when(t == 3)
        def _():
            first_wait(1, 3, 4)
            first_start(1, 7, 8)
            first_sent(0)

        later = turn(t + 1)

        @pl.when(later < units)
        def _():
            pick(0, later)

        @pl.when(t + 1 == early)
        def _():
            first_wait(1, 5, 6, 7, 8)

        @pl.when((later >= units) & (t + 1 < steps))
        def _():
            pick(1, later - units)

        @pl.when(t + 1 < steps)
        def _():
            second_start(t + 1, 0, 1, 2)

        @pl.when(t == units)
        def _():
            first_sent(1)

        @pl.when(t < steps)
        def _():
            second_wait(t, 1, 2)
            second_start(t, 5, 6)
            second_wait(t, 0)
            second_start(t, 3, 4)

        @pl.when((t >= 1) & (t < steps + 1))
        def _():
            second_wait(t - 1, 5, 6)
            second_start(t - 1, 7)

        @pl.when((t >= 2) & (t < steps + 2))
        def _():
            second_wait(t - 2, 3, 4, 7)
            second_start(t - 2, 8)

        ready = turn(t - 3)

        @pl.when((t >= 3) & (ready < units))
        def _():
            second_wait(t - 3, 8)
            multiply(0, ready)

        @pl.when(ready >= units)
        def _():
            second_wait(t - 3, 8)
            multiply(1, ready - units)

        @pl.when(t == early + 3)
        def _():
            third_start(0, 1, 2)

        @pl.when(t == early + 5)
        def _():
            third_wait(1, 2)
            third_start(5, 6)
            third_wait(0)
            third_start(3, 4)

        @pl.when(t == early + 8)
        def _():
            third_wait(3, 4)
            third_start(7, 8)

        @pl.when(t >= 5)
        def _():
            second_sent(t - 5)

        return carry

    lax.fori_loop(0, steps + 3, step, 0)
    third_wait(7, 8)
    keep(y_other + z_far).start()
    for r in range(pool.shape[0]):
        keep(r).wait()
    for kind, (ref, to) in enumerate(third_out):
        third(kind, ref, to).wait_send()
    store(units - 2).wait()
    store(units - 1).wait()
    second_sent(steps - 2)
    second_sent(steps - 1)


def run_gather_project(size, order, idx, tokens, weight, gain):
    row_count = lax.axis_size("row")
    groups = tokens.shape[0]
    count = size // UNITS
    width = weight.shape[1] * weight.shape[2]
    depth = weight.shape[0]
    return pl.pallas_call(
        functools.partial(gather_project, UNITS),
        out_shape=jax.ShapeDtypeStruct((size + row_count * count // 2,) + weight.shape[1:], jnp.bfloat16),
        in_specs=[
            pl.BlockSpec(memory_space=pltpu.SMEM),
            pl.BlockSpec(memory_space=pl.ANY),
            pl.BlockSpec(memory_space=pl.ANY),
            pl.BlockSpec(memory_space=VMEM),
        ],
        out_specs=pl.BlockSpec(memory_space=pl.ANY),
        scratch_shapes=[
            VMEM((row_count * groups, GROUP, 128), jnp.bfloat16),
            VMEM((row_count * groups, GROUP, 128), jnp.bfloat16),
            VMEM((2, 2, 8, size, 128), jnp.bfloat16),
            VMEM((2, depth // 2, width), jnp.bfloat16),
            VMEM((size, width), jnp.bfloat16),
            VMEM((2, 256) + weight.shape[1:], jnp.bfloat16),
            VMEM((2, count) + weight.shape[1:], jnp.bfloat16),
            VMEM((row_count, count // 2) + weight.shape[1:], jnp.bfloat16),
            pltpu.SemaphoreType.DMA((4,)),
            pltpu.SemaphoreType.DMA((2, 9)),
            pltpu.SemaphoreType.DMA((2, 9)),
            pltpu.SemaphoreType.DMA((2 * UNITS, 9)),
            pltpu.SemaphoreType.DMA((2 * UNITS, 9)),
            pltpu.SemaphoreType.DMA((9,)),
            pltpu.SemaphoreType.DMA((9,)),
            pltpu.SemaphoreType.DMA((row_count,)),
            pltpu.SemaphoreType.DMA((2,)),
        ],
        compiler_params=pltpu.CompilerParams(
            collective_id=order, has_side_effects=True, vmem_limit_bytes=60 * 2**20),
        name=f"gather_project_{size}",
    )(idx, tokens, weight, gain)


def lay_out(table, kv, out, held, zeros, load_sem, sem, zero_sem):
    samples, plen = out.shape[0], out.shape[1]

    def load(s):
        n = table[1, s]
        return pltpu.make_async_copy(kv.at[pl.ds(table[0, s], n)], held.at[s, pl.ds(0, n)], load_sem.at[s])

    def rows(s):
        n = table[1, s]
        return pltpu.make_async_copy(held.at[s, pl.ds(0, n)], out.at[s, pl.ds(0, n)], sem.at[s])

    def rest(s):
        n = table[1, s]
        return pltpu.make_async_copy(zeros.at[pl.ds(0, plen - n)], out.at[s, pl.ds(n, plen - n)], zero_sem.at[s])

    for s in range(samples):
        load(s).start()
    zeros[...] = jnp.zeros_like(zeros)
    for s in range(samples):
        @pl.when(table[1, s] < plen)
        def _():
            rest(s).start()

    for s in range(samples):
        load(s).wait()
        rows(s).start()
    for s in range(samples):
        rows(s).wait()

        @pl.when(table[1, s] < plen)
        def _():
            rest(s).wait()


def run_lay_out(table, samples, kv):
    return pl.pallas_call(
        lay_out,
        out_shape=jax.ShapeDtypeStruct((samples, PLEN) + kv.shape[1:], kv.dtype),
        in_specs=[
            pl.BlockSpec(memory_space=pltpu.SMEM),
            pl.BlockSpec(memory_space=pl.ANY),
        ],
        out_specs=pl.BlockSpec(memory_space=pl.ANY),
        scratch_shapes=[
            VMEM((samples, PLEN) + kv.shape[1:], kv.dtype),
            VMEM((PLEN,) + kv.shape[1:], kv.dtype),
            pltpu.SemaphoreType.DMA((samples,)),
            pltpu.SemaphoreType.DMA((samples,)),
            pltpu.SemaphoreType.DMA((samples,)),
        ],
        name="lay_out",
    )(table, kv)


def any_size(tokens, norm_gain, projection, first_token, passage_len):
    rows_here, columns = tokens.shape
    model_width = columns * lax.axis_size("head")
    pair_count, inner_dev = (projection.shape[1], projection.shape[2])
    flat_weight = projection.reshape(model_width, pair_count * inner_dev)
    gathered = lax.all_gather(tokens, "head", axis=1, tiled=True)
    widened = gathered.astype(jnp.float32)
    inverse = lax.rsqrt(jnp.mean(widened * widened, axis=1, keepdims=True) + epsilon)
    normed = (widened * inverse * norm_gain[None, :]).astype(jnp.bfloat16)
    projected = jnp.dot(normed, flat_weight, preferred_element_type=jnp.float32)
    kv_rows = projected.astype(jnp.bfloat16).reshape(rows_here, pair_count, inner_dev)
    everything = lax.all_gather(kv_rows, "row", axis=0, tiled=True)
    positions = jnp.arange(PLEN, dtype=jnp.int32)
    target = first_token[:, None] + positions[None, :]
    filled = positions[None, :] < passage_len[:, None]
    picked = jnp.take(everything, jnp.clip(target, 0, everything.shape[0] - 1), axis=0)
    return jnp.where(filled[:, :, None, None], picked, jnp.zeros((), jnp.bfloat16))


def plan(row_count, lengths, sample_passage, idx, table, match):
    blocks, per_block = lengths.shape
    samples = sample_passage.shape[1]
    here = samples // row_count
    passages = blocks * per_block
    f32 = jnp.float32
    row = lax.axis_index("row")
    mine = row.astype(f32)

    def iota(shape, axis):
        return lax.broadcasted_iota(jnp.int32, shape, axis)

    square = (128, 128)
    diagonal = iota(square, 0) == iota(square, 1)
    before = iota(square, 1) < iota(square, 0)
    lane = iota((1, 128), 1)

    def down(value):
        return jnp.sum(jnp.where(diagonal, value, 0.0), axis=1, keepdims=True)

    def along(value):
        return jnp.sum(jnp.where(diagonal, value, 0.0), axis=0, keepdims=True)

    length = jnp.zeros((1, 128), f32)
    spot = iota((per_block, 128), 1) - iota((per_block, 128), 0)
    for b in range(blocks):
        column = jnp.sum(jnp.where(iota((per_block, per_block), 0) == iota((per_block, per_block), 1),
                                   lengths[b:b + 1, :].astype(f32), 0.0), axis=1, keepdims=True)
        length = length + jnp.sum(jnp.where(spot == b * per_block, column, 0.0), axis=0, keepdims=True)
    offset_d = jnp.sum(jnp.where(before, length, 0.0), axis=1, keepdims=True)
    offset = along(offset_d)
    begin = jnp.floor(offset / GROUP)
    groups = jnp.where(lane < passages, jnp.floor((offset + length - 1.0) / GROUP) - begin + 1.0, 0.0)
    begin_d, groups_d = down(begin), down(groups)

    asked = sample_passage[...].astype(f32)
    same = iota((samples, samples), 0) == iota((samples, samples), 1)
    asked_d = jnp.sum(jnp.where(same, asked, 0.0), axis=1, keepdims=True)
    match[...] = (asked_d == iota((samples, 128), 1).astype(f32)).astype(f32)
    flags = jnp.concatenate(
        [jnp.max(match[r * here:(r + 1) * here, :], axis=0, keepdims=True) for r in range(row_count)], axis=0)
    load = jnp.sum(flags * groups, axis=1, keepdims=True)
    ratio = load / jnp.max(load)
    weight = (ratio * ratio) * (ratio * ratio)
    score = jnp.sum(flags * weight, axis=0, keepdims=True)
    score_d = down(score)
    above = (score > score_d) | ((score == score_d) & before)
    pool_ahead_d = jnp.sum(jnp.where(above, groups, 0.0), axis=1, keepdims=True)
    pool_ahead = along(pool_ahead_d)

    tier = jnp.full((1, 1), float(len(SIZES)), f32)
    share = jnp.zeros((1, 1), f32)
    for number in reversed(range(len(SIZES))):
        part = SIZES[number] // (2 * UNITS * GROUP)
        alone = jnp.where(pool_ahead + groups <= float(part * row_count), 0.0, flags * groups)
        most = jnp.max(jnp.sum(alone, axis=1, keepdims=True), axis=0, keepdims=True)
        fits = most + part <= float(SIZES[number] // GROUP)
        tier = jnp.where(fits, float(number), tier)
        share = jnp.where(fits, float(part), share)

    pooled = pool_ahead + groups <= share * row_count
    pooled_d = pool_ahead_d + groups_d <= share * row_count
    flag_own = jnp.sum(jnp.where(iota((row_count, 128), 0) == row, flags, 0.0), axis=0, keepdims=True)
    number = jnp.where(pooled, 0.0, flag_own * groups)
    number_d = down(number)
    ahead_d = share + jnp.sum(jnp.where(before, number, 0.0), axis=1, keepdims=True)
    slots = idx.shape[1]
    slot = iota((1, slots), 1).astype(f32)
    pool_slot = jnp.where(slot < share, slot + mine * share, -1.0)
    alone = (slot >= ahead_d) & (slot < ahead_d + number_d)
    common = pooled_d & (pool_slot >= pool_ahead_d) & (pool_slot < pool_ahead_d + groups_d)
    value = jnp.where(alone, begin_d + (slot - ahead_d), 0.0) + jnp.where(common, begin_d + (pool_slot - pool_ahead_d), 0.0)
    idx[...] = jnp.sum(value, axis=0, keepdims=True).astype(jnp.int32)

    place = jnp.where(pooled, pool_ahead, share * row_count + along(ahead_d)) * GROUP + (offset - begin * GROUP)
    own_match = match[pl.ds(pl.multiple_of(row * here, 8), here), :]
    lined = iota((here, 128), 0) == iota((here, 128), 1)

    def of_sample(value):
        found = jnp.sum(own_match * value, axis=1, keepdims=True)
        return jnp.sum(jnp.where(lined, found, 0.0), axis=0, keepdims=True)

    rows = [of_sample(place), of_sample(length), of_sample(offset), jnp.broadcast_to(tier, (1, 128))]
    table[...] = jnp.concatenate(rows + rows, axis=0).astype(jnp.int32)


def run_plan(lengths, sample_passage, row_count):
    return pl.pallas_call(
        functools.partial(plan, row_count),
        out_shape=(jax.ShapeDtypeStruct((1, 512), jnp.int32), jax.ShapeDtypeStruct((8, 128), jnp.int32)),
        in_specs=[pl.BlockSpec(memory_space=VMEM)] * 2,
        out_specs=(pl.BlockSpec(memory_space=VMEM), pl.BlockSpec(memory_space=VMEM)),
        scratch_shapes=[VMEM((sample_passage.shape[1], 128), jnp.float32)],
        compiler_params=pltpu.CompilerParams(vmem_limit_bytes=8 * 2**20),
        name="plan",
    )(lengths, sample_passage)


def shards(tokens, norm_gain, projection, lengths, sample_passage):
    columns = tokens.shape[1]
    row_count = lax.axis_size("row")
    samp_here = sample_passage.shape[0] // row_count
    idx, table = run_plan(lengths, sample_passage.reshape(1, -1), row_count)

    def sized(number_of, size):
        def branch():
            kv = run_gather_project(size, number_of, idx, tokens.reshape(-1, GROUP, columns), projection,
                                    norm_gain.reshape(-1, 128))
            return run_lay_out(table, samp_here, kv)

        return branch

    def rest():
        return any_size(tokens, norm_gain, projection, table[2, :samp_here], table[1, :samp_here])

    branches = [sized(i, size) for i, size in enumerate(SIZES)] + [rest]
    return lax.switch(table[3, 0], branches)


def solution(mesh):
    in_specs = (P("row", "head"), P(), P(None, None, "head"), P(), P())
    out_specs = P("row", None, None, "head")
    return jax.shard_map(shards, mesh=mesh, in_specs=in_specs, out_specs=out_specs, check_vma=False)
```
